32 devices in a mesh: region: 8 (over y, x, core), species: 4 (over z).
Axes of the slice: x: 2, y: 2, z: 4, core: 2. Of those that a mesh axis runs over, the one named last changes fastest.
Arguments:
- concentrations: float32 [256, 1024, 256], P('species', 'region'), may hold values from 0.05 to 5
- diffusion: float32 [256], P('species'), may hold values from 0.02 to 0.08
- courant_x: float32 [1024, 256], P('region'), may hold values from -0.2 to 0.2
- courant_y: float32 [1024, 256], P('region'), may hold values from -0.2 to 0.2
- log_rate: float32 [4, 768], replicated, may hold values from -3 to 0
- reactants: int32 [256, 768], replicated, may hold values from 0 to 1, as said below
- products: int32 [768, 256], replicated, may hold values from 0 to 1, as said below
- block_class: int32 [2048], P(('region', 'species')), may hold values from 0 to 3, as said below
- send_slot: int32 [2048], P(('region', 'species')), may hold values from -1 to 15, as said below
Outputs:
- reacted: float32 [256, 1024, 256], P('species', 'region')
The draws below stay inside these ranges and needn't reach their ends.
Inputs may be any that keep to these rules, and one draw needn't show every extreme that they name: `send_slot`: block n lies on the device with region index n // 256 and species index (n // 64) % 4. A value t >= 0 marks a stiff block and names slot t % 2 of region t // 2; -1 marks the others. Among the blocks of one species index every value from 0 to 15 occurs exactly once; for each species index one device holds exactly 8 marked blocks, and no device holds more. The marked blocks of one device name different regions. `block_class`: A block marked in send_slot has class 3; every other block has a lower class. `reactants`: every column has one or two ones, in different rows. `products`: every row has one or two ones, in different columns.
All inputs are finite; a program needn't handle non-finite values.
Results may differ from the reference program's by a relative error of at most 0.0003.
Values sent between devices are 32-bit elements; how exact they have to be, the bound alone decides.
A program may use at most 192 MiB of HBM per device.

```python
import math
import jax
import jax.numpy as jnp
from jax import lax

SPECIES = 256
REACT = 768
CX = 128
NY = 256
STEPS = 3
ITERS = 2
SUB = 2
CLASSES = 4
QUEUE = 2
STIFF_MOST = 8
NX = 1024
N_REGION = 8
N_SPECIES = 4


def stiff_plan(key):
    blocks_dev = CX * NY // (128 * N_SPECIES)
    total = N_REGION * QUEUE
    base = jax.random.fold_in(key, 7001)
    keys = jax.random.split(base, 5)
    heaviest = jax.random.randint(keys[0], (N_SPECIES,), 0, N_REGION)
    others = jax.random.randint(keys[1], (N_SPECIES, total), 0, N_REGION - 1)
    units = jnp.arange(total)
    region_of = jnp.where(units[None, :] < STIFF_MOST, heaviest[:, None], (heaviest[:, None] + 1 + others) % N_REGION)
    earlier = units[None, :, None] > units[None, None, :]
    same_region = region_of[:, :, None] == region_of[:, None, :]
    ranks = jnp.sum((same_region & earlier).astype(jnp.int32), axis=2)
    scores = jax.random.randint(keys[2], (N_SPECIES, N_REGION, blocks_dev), 0, 2 ** 20)
    orders = jnp.argsort(scores * blocks_dev + jnp.arange(blocks_dev), axis=-1).astype(jnp.int32)
    groups = jnp.broadcast_to(jnp.arange(N_SPECIES)[:, None], (N_SPECIES, total))
    block_of = orders[groups, region_of, ranks]
    sorted_units = jnp.argsort(region_of * total + units[None, :], axis=-1).astype(jnp.int32)
    position = jnp.argsort(sorted_units, axis=-1).astype(jnp.int32)
    rotation = jax.random.randint(keys[3], (N_SPECIES, 1), 0, N_REGION)
    label_scores = jax.random.randint(keys[4], (N_SPECIES, N_REGION), 0, 2 ** 20)
    labels = jnp.argsort(label_scores * N_REGION + jnp.arange(N_REGION)[None, :], axis=-1).astype(jnp.int32)
    target = jnp.take_along_axis(labels, (position + rotation) % N_REGION, axis=1)
    slot_of = (target * QUEUE + position // N_REGION).astype(jnp.int32)
    return (region_of, groups, block_of, slot_of)


def draw_send_slot(key, part):
    blocks_dev = CX * NY // (128 * N_SPECIES)
    region_of, groups, block_of, slot_of = stiff_plan(key)
    layout = jnp.full((N_REGION, N_SPECIES, blocks_dev), -1, jnp.int32)
    layout = layout.at[region_of, groups, block_of].set(slot_of)
    return layout.reshape(-1)


def draw_block_class(key, part):
    blocks_dev = CX * NY // (128 * N_SPECIES)
    region_of, groups, block_of, slot_of = stiff_plan(key)
    lower = jax.random.randint(jax.random.fold_in(key, 7002), (N_REGION, N_SPECIES, blocks_dev), 0, CLASSES - 1)
    layout = lower.at[region_of, groups, block_of].set(CLASSES - 1)
    return layout.reshape(-1).astype(jnp.int32)


def pair_table(key, salt):
    keys = jax.random.split(jax.random.fold_in(key, salt), 3)
    first_pick = jax.random.randint(keys[0], (REACT,), 0, SPECIES)
    offset = jax.random.randint(keys[1], (REACT,), 1, SPECIES)
    second_pick = (first_pick + offset) % SPECIES
    doubled = jax.random.randint(keys[2], (REACT,), 0, 2)
    species_ids = jnp.arange(SPECIES)[:, None]
    chosen = (species_ids == first_pick[None, :]) | (species_ids == second_pick[None, :]) & (doubled[None, :] == 1)
    return chosen.astype(jnp.int32)


def draw_reactants(key, part):
    return pair_table(key, 7101)


def draw_products(key, part):
    return pair_table(key, 7201).T


def block_levels(own_key, shape, cuts, low, largest):
    gain = 1.0
    for dim, parts in cuts:
        heights = jax.random.uniform(jax.random.fold_in(jax.random.fold_in(own_key, 6), dim), (parts,), jnp.float32, low / len(cuts), largest / len(cuts))
        gain = gain * jnp.repeat(jnp.exp(heights), shape[dim] // parts).reshape((-1,) + (1,) * (len(shape) - 1 - dim))
    return gain


def setup_inputs(seed: int = 0) -> dict:
    seeds = jax.random.split(jax.random.key(seed), 10)
    concentrations = jnp.clip(jnp.exp(math.log(5.0) - 4.6051702 * jax.random.uniform(seeds[0], (SPECIES, NX, NY), jnp.float32) ** block_levels(seeds[0], (SPECIES, NX, NY), ((0, 4), (1, 8)), -0.2, 0.2)), 0.05, 5.0)
    diffusion = jnp.clip(0.02 + 0.06 * jax.random.uniform(seeds[1], (SPECIES,), jnp.float32) ** block_levels(seeds[1], (SPECIES,), ((0, 4),), -0.2, 0.2), 0.02, 0.08)
    courant_x = jnp.clip(jax.random.uniform(seeds[2], (NX, NY), jnp.float32, -0.2, 0.2) * block_levels(seeds[2], (NX, NY), ((0, 8),), -0.4, 0.0), -0.2, 0.2)
    courant_y = jnp.clip(jax.random.uniform(seeds[3], (NX, NY), jnp.float32, -0.2, 0.2) * block_levels(seeds[3], (NX, NY), ((0, 8),), -0.4, 0.0), -0.2, 0.2)
    log_rate = jnp.clip(jax.random.uniform(seeds[4], (CLASSES, REACT), jnp.float32, -3.0, 0.0), -3.0, 0.0)
    reactants = draw_reactants(jax.random.fold_in(seeds[9], 71), 0)
    products = draw_products(jax.random.fold_in(seeds[9], 71), 0)
    block_class = draw_block_class(jax.random.fold_in(seeds[9], 71), 0)
    send_slot = draw_send_slot(jax.random.fold_in(seeds[9], 71), 0)
    return {"concentrations": concentrations, "diffusion": diffusion, "courant_x": courant_x, "courant_y": courant_y, "log_rate": log_rate, "reactants": reactants, "products": products, "block_class": block_class, "send_slot": send_slot}


floor_value = 0.05
highest = lax.Precision.HIGHEST


def minmod(first_diff, second):
    signed = jnp.sign(first_diff)
    return signed * jnp.maximum(0.0, jnp.minimum(jnp.abs(first_diff), signed * second))


def face_flux(field, courant, diffuse, axis_index):
    length = field.shape[axis_index]
    behind = lax.slice_in_dim(field, 0, length - 3, axis=axis_index)
    center = lax.slice_in_dim(field, 1, length - 2, axis=axis_index)
    forward = lax.slice_in_dim(field, 2, length - 1, axis=axis_index)
    beyond = lax.slice_in_dim(field, 3, length, axis=axis_index)
    upwind = center + 0.5 * (1.0 - courant) * minmod(center - behind, forward - center)
    downwind = forward - 0.5 * (1.0 + courant) * minmod(forward - center, beyond - forward)
    return courant * jnp.where(courant >= 0.0, upwind, downwind) - diffuse * (forward - center)


def substep(padded, wind_rows, cross_rows, diffuse):
    height = padded.shape[1]
    row_faces = 0.5 * (wind_rows[1:height - 2] + wind_rows[2:height - 1])
    flux_rows = face_flux(padded, row_faces[None], diffuse, 1)
    interior = padded[:, 2:height - 2]
    widened = jnp.pad(interior, ((0, 0), (0, 0), (2, 2)))
    cross_pad = jnp.pad(cross_rows, ((0, 0), (2, 2)))
    extent = cross_pad.shape[1]
    across = 0.5 * (cross_pad[:, 1:extent - 2] + cross_pad[:, 2:extent - 1])
    flux_cols = face_flux(widened, across[None], diffuse, 2)
    return interior - (flux_rows[:, 1:] - flux_rows[:, :-1]) - (flux_cols[:, :, 1:] - flux_cols[:, :, :-1])


def backward_euler(anchor, rate_logs, reactant_coef, product_coef, stride):
    iterate = anchor
    for iteration in range(ITERS):
        summed = lax.dot_general(reactant_coef, jnp.log(iterate), (((0,), (0,)), ((), ())), precision=highest, preferred_element_type=jnp.float32)
        reaction_rates = jnp.exp(rate_logs + summed)
        making = lax.dot_general(product_coef, reaction_rates, (((0,), (0,)), ((), ())), precision=highest, preferred_element_type=jnp.float32)
        losing = jnp.dot(reactant_coef, reaction_rates, precision=highest, preferred_element_type=jnp.float32)
        iterate = (anchor + stride * making) / (1.0 + stride * losing / iterate)
    return iterate


def stiff_steps(anchor, rate_logs, reactant_coef, product_coef):
    iterate = anchor
    for counter in range(SUB):
        iterate = backward_euler(iterate, rate_logs, reactant_coef, product_coef, 1.0 / SUB)
    return iterate


def reference(concentrations, diffusion, courant_x, courant_y, log_rate, reactants, products, block_class, send_slot):
    group_size = SPECIES // N_SPECIES
    wind_pad = jnp.pad(courant_x, ((2, 2), (0, 0)))

    def transport(pieces):
        concentration, spread = pieces
        diffuse = spread[:, None, None]
        for counter in range(STEPS):
            concentration = substep(jnp.pad(concentration, ((0, 0), (2, 2), (0, 0))), wind_pad, courant_y, diffuse)
        return concentration

    advected = lax.map(transport, (concentrations.reshape(N_SPECIES, group_size, NX, NY), diffusion.reshape(N_SPECIES, group_size)))
    piece_cells = CX * NY // N_SPECIES
    piece_count = NX * NY // piece_cells
    pieces_conc = advected.reshape(SPECIES, piece_count, piece_cells).transpose(1, 0, 2)
    cell_class = jnp.repeat(block_class, 128).reshape(piece_count, piece_cells)
    stiff_flags = jnp.repeat(send_slot >= 0, 128).reshape(piece_count, piece_cells)
    reactant_coef = reactants.astype(jnp.float32)
    product_coef = products.astype(jnp.float32)
    rate_table = log_rate.T

    def react(pieces):
        values, classes, flags = pieces
        anchor = jnp.maximum(values, floor_value)
        rate_logs = rate_table[:, classes]
        single_step = backward_euler(anchor, rate_logs, reactant_coef, product_coef, 1.0)
        multi_step = stiff_steps(anchor, rate_logs, reactant_coef, product_coef)
        return jnp.where(flags[None, :], multi_step, single_step)

    reacted = lax.map(react, (pieces_conc, cell_class, stiff_flags))
    return reacted.transpose(1, 0, 2).reshape(SPECIES, NX, NY)
```

```python
import functools

import jax
import jax.numpy as jnp
from jax import lax
from jax.experimental import pallas as pl
from jax.experimental.pallas import tpu as pltpu
from jax.sharding import PartitionSpec as P

STEPS = 3
ITERS = 2
SUB = 2
HALO = 2 * STEPS
BLOCK = 128
FLOOR = 0.05


def minmod(p, r):
    return jnp.maximum(jnp.minimum(p, r), 0.0) + jnp.minimum(jnp.maximum(p, r), 0.0)


def flux(a, am, e, nu, q0, before, here, after):
    m = minmod(here, jnp.where(a >= 0.0, before, after))
    return a * q0 + (am - nu) * here + e * m


def transport_kernel(n, ids, x, top, bottom, nu_ref, coef, *rest):
    outs, buf = rest[:n], rest[n]
    _, rows, cols = x.shape
    total = rows + 2 * HALO
    for r in range(HALO):
        buf[r] = top[:, r, :]
        buf[HALO + rows + r] = bottom[:, r, :]

    def turn(g, carry):
        at = pl.multiple_of(g * 8, 8)
        buf[pl.ds(HALO + at, 8)] = jnp.swapaxes(x[:, pl.ds(at, 8), :], 0, 1)
        return carry

    lax.fori_loop(0, rows // 8, turn, 0)
    nu = nu_ref[...]
    lane = lax.broadcasted_iota(jnp.int32, (8, cols), 1)
    first, last = lane == 0, lane == cols - 1

    def c(e, k):
        return jnp.broadcast_to(coef[e, k : k + 1, :], (8, cols))

    def face(e, q0, before, here, after):
        return flux(c(e, 0), c(e, 1), c(e, 2), nu, q0, before, here, after)

    for step in range(STEPS):
        lo, hi = 2 * (step + 1), total - 2 * (step + 1)
        qa, qb, qc, qd = buf[lo - 2], buf[lo - 1], buf[lo], buf[lo + 1]
        start = face(lo - 1, qb, qb - qa, qc - qb, qd - qc)

        def body(e, carry):
            q0, q1, before, here, prev = carry
            q2 = buf[e + 2]
            after = q2 - q1
            f = face(e, q0, before, here, after)
            right = jnp.where(last, 0.0, pltpu.roll(q0, cols - 1, 1))
            d = right - q0
            dm = jnp.where(first, q0, pltpu.roll(d, 1, 1))
            dp = jnp.where(last, 0.0, pltpu.roll(d, cols - 1, 1))
            g = flux(c(e, 3), c(e, 4), c(e, 5), nu, q0, dm, d, dp)
            edge = (c(e, 6) - nu) * q0 + c(e, 7) * minmod(q0, d)
            gl = jnp.where(first, edge, pltpu.roll(g, 1, 1))
            buf[e] = q0 - (f - prev) - (g - gl)
            return q1, q2, here, after, f

        lax.fori_loop(lo, hi, body, (qc, qd, qc - qb, qd - qc, start), unroll=4)
        if step < STEPS - 1:
            zeros = jnp.zeros((HALO, 8, cols), jnp.float32)

            @pl.when(ids[1] == 0)
            def _():
                buf[0:HALO] = zeros

            @pl.when(ids[1] == ids[2] - 1)
            def _():
                buf[HALO + rows : total] = zeros

    own = rows // n
    for s in range(n):
        owner = lax.rem(ids[0] + s, n)
        outs[s][...] = buf[pl.ds(HALO + owner * own, own)]


def transport(ids, conc, top, bottom, nu, coef, n, chunk, index):
    _, rows, cols = conc.shape
    own = rows // n
    base = index * (chunk // 8)
    return pl.pallas_call(
        functools.partial(transport_kernel, n),
        name=f"transport{index}",
        grid_spec=pltpu.PrefetchScalarGridSpec(
            num_scalar_prefetch=1,
            grid=(chunk // 8,),
            in_specs=[
                pl.BlockSpec((8, rows, cols), lambda i, ids: (base + i, 0, 0)),
                pl.BlockSpec((8, HALO, cols), lambda i, ids: (i, 0, 0)),
                pl.BlockSpec((8, HALO, cols), lambda i, ids: (i, 0, 0)),
                pl.BlockSpec((8, cols), lambda i, ids: (base + i, 0)),
                pl.BlockSpec(coef.shape, lambda i, ids: (0, 0, 0)),
            ],
            out_specs=[pl.BlockSpec((own, 8, cols), lambda i, ids: (0, i, 0))] * n,
            scratch_shapes=[pltpu.VMEM((rows + 2 * HALO, 8, cols), jnp.float32)],
        ),
        out_shape=[jax.ShapeDtypeStruct((own, chunk, cols), jnp.float32)] * n,
        compiler_params=pltpu.CompilerParams(vmem_limit_bytes=48 << 20),
        cost_estimate=pl.CostEstimate(
            flops=chunk * rows * cols * 160,
            bytes_accessed=chunk * rows * cols * 8,
            transcendentals=0,
        ),
    )(ids, conc, top, bottom, nu, coef)


def chemistry_kernel(n, parts, first, classes, slots, *rest):
    pieces = rest[: n * parts]
    first_table, second_table, logs = rest[n * parts : n * parts + 3]
    outs = rest[n * parts + 3 : n * parts + 3 + n]
    anchor, state, lifted, rated, kept = rest[n * parts + 3 + n :]
    rows, chunk, cols = pieces[0].shape
    group = chunk * parts
    species = group * n
    reactions = logs.shape[1]
    per_row = cols // BLOCK

    def iterate(lanes, stride):
        g = state[:, lanes]
        lg = jnp.log(g)
        hi = lg.astype(jnp.bfloat16)
        lifted[:species, lanes] = hi
        lifted[species:, lanes] = (lg - hi.astype(jnp.float32)).astype(jnp.bfloat16)
        summed = jnp.dot(first_table[...], lifted[:, lanes], preferred_element_type=jnp.float32)
        rate = jnp.exp(kept[:, lanes] + summed)
        hi = rate.astype(jnp.bfloat16)
        rated[:reactions, lanes] = hi
        rated[reactions:, lanes] = (rate - hi.astype(jnp.float32)).astype(jnp.bfloat16)
        both = jnp.dot(second_table[...], rated[:, lanes], preferred_element_type=jnp.float32)
        g = state[:, lanes]
        top = anchor[:, lanes] + stride * both[:species]
        state[:, lanes] = top / (1.0 + stride * both[species:] / g)

    whole = slice(0, cols)

    def one_row(r, carry):
        block = (first + pl.program_id(0) * rows + r) * per_row
        for b in range(per_row):
            kept[:, b * BLOCK : (b + 1) * BLOCK] = logs[classes[block + b]]
        for p in range(n * parts):
            start = jnp.maximum(pieces[p][r], FLOOR)
            anchor[p * chunk : (p + 1) * chunk, :] = start
            state[p * chunk : (p + 1) * chunk, :] = start

        def step(_, c):
            iterate(whole, 1.0)
            return c

        lax.fori_loop(0, ITERS, step, 0)
        for b in range(per_row):
            lanes = slice(b * BLOCK, (b + 1) * BLOCK)

            @pl.when(slots[block + b] >= 0)
            def _():
                state[:, lanes] = anchor[:, lanes]

                def sub(_, c):
                    anchor[:, lanes] = state[:, lanes]

                    def step(_, c2):
                        iterate(lanes, 1.0 / SUB)
                        return c2

                    return lax.fori_loop(0, ITERS, step, c)

                lax.fori_loop(0, SUB, sub, 0)

        for s in range(n):
            outs[s][r] = state[s * group : (s + 1) * group, :]
        return carry

    lax.fori_loop(0, rows, one_row, 0)


def chemistry(classes, slots, pieces, tables, logs, n, parts, first, count, step, index):
    _, chunk, cols = pieces[0].shape
    group = chunk * parts
    species = group * n
    reactions = logs.shape[1]
    base = first // step

    def fixed(shape):
        return pl.BlockSpec(
            shape, lambda i, *_: (0,) * len(shape), pipeline_mode=pl.Buffered(1)
        )

    return pl.pallas_call(
        functools.partial(chemistry_kernel, n, parts, first),
        name=f"chemistry{index}",
        grid_spec=pltpu.PrefetchScalarGridSpec(
            num_scalar_prefetch=2,
            grid=(count // step,),
            in_specs=[pl.BlockSpec((step, chunk, cols), lambda i, *_: (base + i, 0, 0))]
            * (n * parts)
            + [fixed(tables[0].shape), fixed(tables[1].shape), fixed(logs.shape)],
            out_specs=[pl.BlockSpec((step, group, cols), lambda i, *_: (i, 0, 0))] * n,
            scratch_shapes=[
                pltpu.VMEM((species, cols), jnp.float32),
                pltpu.VMEM((species, cols), jnp.float32),
                pltpu.VMEM((2 * species, cols), jnp.bfloat16),
                pltpu.VMEM((2 * reactions, cols), jnp.bfloat16),
                pltpu.VMEM((reactions, cols), jnp.float32),
            ],
        ),
        out_shape=[jax.ShapeDtypeStruct((count, group, cols), jnp.float32)] * n,
        compiler_params=pltpu.CompilerParams(vmem_limit_bytes=48 << 20),
        cost_estimate=pl.CostEstimate(
            flops=count * cols * species * reactions * 2 * 6 * ITERS,
            bytes_accessed=count * cols * species * 8,
            transcendentals=count * cols * (species + reactions) * ITERS,
        ),
    )(classes, slots, *pieces, *tables, logs)


def assemble_kernel(n, per, aliased, ids, *rest):
    pieces = rest[aliased : aliased + n * per]
    out = rest[-1]
    group = out.shape[0]
    at = pl.program_id(0)
    for s in range(n):

        @pl.when(at == s)
        def _():
            mine = pieces[s * per : (s + 1) * per]

            def turn(q, carry):
                sp = pl.ds(pl.multiple_of(q * 8, 8), 8)
                parts = [p[:, sp, :] for p in mine]
                v = parts[0] if per == 1 else jnp.concatenate(parts, axis=0)
                out[sp] = jnp.swapaxes(v, 0, 1)
                return carry

            lax.fori_loop(0, group // 8, turn, 0)


def assemble(ids, pieces, per, previous, shape, n, row):
    group, rows, cols = shape
    own = rows // n // 8
    aliased = 0 if previous is None else 1
    row_block = row // 8
    specs = [
        pl.BlockSpec(p.shape, lambda i, ids: (0, 0, 0), pipeline_mode=pl.Buffered(1))
        for p in pieces
    ]
    return pl.pallas_call(
        functools.partial(assemble_kernel, n, per, aliased),
        name=f"assemble{row}",
        grid_spec=pltpu.PrefetchScalarGridSpec(
            num_scalar_prefetch=1,
            grid=(n,),
            in_specs=[pl.BlockSpec(memory_space=pl.ANY)] * aliased + specs,
            out_specs=pl.BlockSpec(
                (group, 8, cols), lambda i, ids: (0, lax.rem(ids[0] + i, n) * own + row_block, 0)
            ),
        ),
        out_shape=jax.ShapeDtypeStruct(shape, jnp.float32),
        input_output_aliases={1: 0} if aliased else {},
        compiler_params=pltpu.CompilerParams(vmem_limit_bytes=32 << 20),
        cost_estimate=pl.CostEstimate(
            flops=group * 8 * n * cols, bytes_accessed=group * 8 * n * cols * 8, transcendentals=0
        ),
    )(ids, *([previous] if aliased else []), *pieces)


def halo(array, dim):
    devices = lax.axis_size("region")
    up = [(i, i + 1) for i in range(devices - 1)]
    down = [(j, i) for i, j in up]
    length = array.shape[dim]
    last = lax.slice_in_dim(array, length - HALO, length, axis=dim)
    leading = lax.slice_in_dim(array, 0, HALO, axis=dim)
    return lax.ppermute(last, "region", up), lax.ppermute(leading, "region", down)


def face_coefficients(courant_x, courant_y):
    winds = jnp.stack([courant_x, courant_y])
    before, after = halo(winds, 1)
    winds = jnp.concatenate([before, winds, after], axis=1)
    cx, cy = winds[0], winds[1]
    ax = 0.5 * (cx + jnp.pad(cx[1:], ((0, 1), (0, 0))))
    ay = 0.5 * (cy + jnp.pad(cy[:, 1:], ((0, 0), (0, 1))))
    left = 0.5 * cy

    def slope(a):
        return a * jnp.where(a >= 0.0, 0.5 * (1.0 - a), -0.5 * (1.0 + a))

    return jnp.stack(
        [
            ax,
            jnp.minimum(ax, 0.0),
            slope(ax),
            ay,
            jnp.minimum(ay, 0.0),
            slope(ay),
            jnp.minimum(left, 0.0),
            jnp.where(left >= 0.0, 0.0, slope(left)),
        ],
        axis=1,
    )


def per_device(conc, diffusion, courant_x, courant_y, log_rate, reactants, products, block_class, send_slot):
    n = lax.axis_size("species")
    group, rows, cols = conc.shape
    me = lax.axis_index("species")
    region = lax.axis_index("region")
    ids = jnp.stack([me, region, jnp.int32(lax.axis_size("region"))]).astype(jnp.int32)
    own = rows // n
    chunk = max(8, group // 4)
    parts = group // chunk

    coef = face_coefficients(courant_x, courant_y)
    nu = jnp.broadcast_to(diffusion[:, None], (group, cols))
    held = [[None] * parts for _ in range(n)]
    for j in range(parts):
        top, bottom = halo(conc[j * chunk : (j + 1) * chunk], 1)
        sent = transport(ids, conc, top, bottom, nu, coef, n, chunk, j)
        held[0][j] = sent[0]
        for s in range(1, n):
            held[s][j] = lax.ppermute(sent[s], "species", [(i, (i + s) % n) for i in range(n)])

    order = lax.rem(me - jnp.arange(n) + n, n)
    reacts = jnp.take(reactants.reshape(n, group, -1), order, axis=0).reshape(n * group, -1)
    makes = jnp.take(products.T.reshape(n, group, -1), order, axis=0).reshape(n * group, -1)
    reacts, makes = reacts.astype(jnp.bfloat16), makes.astype(jnp.bfloat16)
    first_table = jnp.concatenate([reacts.T, reacts.T], axis=1)
    second = jnp.concatenate([makes, reacts], axis=0)
    second_table = jnp.concatenate([second, second], axis=1)
    logs = jnp.broadcast_to(log_rate[:, :, None], log_rate.shape + (BLOCK,))

    pieces = [held[s][j] for s in range(n) for j in range(parts)]
    step = 4
    counts = [4, 4] + [8] * (own // 8 - 1)
    result, at, waiting = None, 0, []
    for k, count in enumerate(counts):
        made = chemistry(
            block_class, send_slot, pieces, (first_table, second_table), logs, n, parts, at, count, step, k
        )
        back = [made[0]]
        for s in range(1, n):
            back.append(lax.ppermute(made[s], "species", [(i, (i - s) % n) for i in range(n)]))
        waiting.append(back)
        at += count
        if at % 8 == 0:
            done = [w[s] for s in range(n) for w in waiting]
            result = assemble(ids, done, len(waiting), result, conc.shape, n, at - 8)
            waiting = []
    return result


def solution(mesh):
    in_specs = (
        P("species", "region", None),
        P("species"),
        P("region", None),
        P("region", None),
        P(),
        P(),
        P(),
        P(("region", "species")),
        P(("region", "species")),
    )
    out_specs = P("species", "region", None)
    return jax.shard_map(per_device, mesh=mesh, in_specs=in_specs, out_specs=out_specs, check_vma=False)
```

```python
import functools

import jax
import jax.numpy as jnp
from jax import lax
from jax.experimental import pallas as pl
from jax.experimental.pallas import tpu as pltpu
from jax.sharding import PartitionSpec as P


STEPS = 3
ITERS = 2
SUB = 2
HALO = 2 * STEPS
BLOCK = 128
FLOOR = 0.05
UNROLL = 4


def minmod(p, r):
    return jnp.maximum(jnp.minimum(p, r), 0.0) + jnp.minimum(jnp.maximum(p, r), 0.0)


def flux(a, am, e, nu, q0, before, here, after):
    m = minmod(here, jnp.where(a >= 0.0, before, after))
    return a * q0 + (am - nu) * here + e * m


def transport_kernel(n, ids, x, top, bottom, nu_ref, coef, *rest):
    outs, buf = rest[:n], rest[n]
    _, rows, cols = x.shape
    total = rows + 2 * HALO
    for r in range(HALO):
        buf[r] = top[:, r, :]
        buf[HALO + rows + r] = bottom[:, r, :]

    def turn(g, carry):
        at = pl.multiple_of(g * 8, 8)
        buf[pl.ds(HALO + at, 8)] = jnp.swapaxes(x[:, pl.ds(at, 8), :], 0, 1)
        return carry

    lax.fori_loop(0, rows // 8, turn, 0)
    nu = nu_ref[...]
    lane = lax.broadcasted_iota(jnp.int32, (8, cols), 1)
    first, last = lane == 0, lane == cols - 1

    def c(e, k):
        return coef[e, pl.ds(k, 8, stride=0), :]

    def face(e, q0, before, here, after):
        return flux(c(e, 0), c(e, 1), c(e, 2), nu, q0, before, here, after)

    for step in range(STEPS):
        lo, hi = 2 * (step + 1), total - 2 * (step + 1)
        qa, qb, qc, qd = buf[lo - 2], buf[lo - 1], buf[lo], buf[lo + 1]
        start = face(lo - 1, qb, qb - qa, qc - qb, qd - qc)

        def body(t, carry):
            e0 = lo + t * UNROLL
            q0, q1, before, here, prev = carry
            ahead = [buf[e0 + u + 2] for u in range(UNROLL)]
            made = []
            for u in range(UNROLL):
                e = e0 + u
                q2 = ahead[u]
                after = q2 - q1
                f = face(e, q0, before, here, after)
                right = jnp.where(last, 0.0, pltpu.roll(q0, cols - 1, 1))
                d = right - q0
                dm = jnp.where(first, q0, pltpu.roll(d, 1, 1))
                dp = jnp.where(last, 0.0, pltpu.roll(d, cols - 1, 1))
                g = flux(c(e, 3), c(e, 4), c(e, 5), nu, q0, dm, d, dp)
                edge = (c(e, 6) - nu) * q0 + c(e, 7) * minmod(q0, d)
                gl = jnp.where(first, edge, pltpu.roll(g, 1, 1))
                made.append(q0 - (f - prev) - (g - gl))
                q0, q1, before, here, prev = q1, q2, here, after, f
            for u in range(UNROLL):
                buf[e0 + u] = made[u]
            return q0, q1, before, here, prev

        lax.fori_loop(0, (hi - lo) // UNROLL, body, (qc, qd, qc - qb, qd - qc, start))
        if step < STEPS - 1:
            zeros = jnp.zeros((HALO, 8, cols), jnp.float32)

            @pl.when(ids[1] == 0)
            def _():
                buf[0:HALO] = zeros

            @pl.when(ids[1] == ids[2] - 1)
            def _():
                buf[HALO + rows : total] = zeros

    own = rows // n
    for s in range(n):
        owner = lax.rem(ids[0] + s, n)
        outs[s][...] = buf[pl.ds(HALO + owner * own, own)]


def transport(ids, conc, top, bottom, nu, coef, n, chunk, offset):
    _, rows, cols = conc.shape
    own = rows // n
    base = offset // 8
    return pl.pallas_call(
        functools.partial(transport_kernel, n),
        grid_spec=pltpu.PrefetchScalarGridSpec(
            num_scalar_prefetch=1,
            grid=(chunk // 8,),
            in_specs=[
                pl.BlockSpec((8, rows, cols), lambda i, ids: (base + i, 0, 0)),
                pl.BlockSpec((8, HALO, cols), lambda i, ids: (base + i, 0, 0)),
                pl.BlockSpec((8, HALO, cols), lambda i, ids: (base + i, 0, 0)),
                pl.BlockSpec((8, cols), lambda i, ids: (base + i, 0)),
                pl.BlockSpec(coef.shape, lambda i, ids: (0, 0, 0)),
            ],
            out_specs=[pl.BlockSpec((own, 8, cols), lambda i, ids: (0, i, 0))] * n,
            scratch_shapes=[pltpu.VMEM((rows + 2 * HALO, 8, cols), jnp.float32)],
        ),
        out_shape=[jax.ShapeDtypeStruct((own, chunk, cols), jnp.float32)] * n,
        compiler_params=pltpu.CompilerParams(vmem_limit_bytes=48 << 20),
        cost_estimate=pl.CostEstimate(
            flops=chunk * rows * cols * 160,
            bytes_accessed=chunk * rows * cols * 8,
            transcendentals=0,
        ),
    )(ids, conc, top, bottom, nu, coef)


def chemistry_kernel(n, parts, first, ordered, classes, slots, *rest):
    rest = rest[ordered:]
    pieces = rest[: n * parts]
    first_table, second_table, logs = rest[n * parts : n * parts + 3]
    outs = rest[n * parts + 3 : n * parts + 3 + n]
    anchor, state, lifted, rated, kept = rest[n * parts + 3 + n :]
    rows, _, cols = pieces[0].shape
    group = outs[0].shape[1]
    species = group * n
    sizes = [p.shape[1] for p in pieces]
    reactions = logs.shape[1]
    per_row = cols // BLOCK

    def iterate(lanes, stride):
        g = state[:, lanes]
        lg = jnp.log(g)
        hi = lg.astype(jnp.bfloat16)
        lifted[:species, lanes] = hi
        lifted[species:, lanes] = (lg - hi.astype(jnp.float32)).astype(jnp.bfloat16)
        summed = jnp.dot(first_table[...], lifted[:, lanes], preferred_element_type=jnp.float32)
        rate = jnp.exp(kept[:, lanes] + summed)
        hi = rate.astype(jnp.bfloat16)
        rated[:reactions, lanes] = hi
        rated[reactions:, lanes] = (rate - hi.astype(jnp.float32)).astype(jnp.bfloat16)
        both = jnp.dot(second_table[...], rated[:, lanes], preferred_element_type=jnp.float32)
        g = state[:, lanes]
        top = anchor[:, lanes] + stride * both[:species]
        state[:, lanes] = top / (1.0 + stride * both[species:] / g)

    whole = slice(0, cols)

    def one_row(r, carry):
        block = (first + pl.program_id(0) * rows + r) * per_row
        for b in range(per_row):
            kept[:, b * BLOCK : (b + 1) * BLOCK] = logs[classes[block + b]]
        for p in range(n * parts):
            start = jnp.maximum(pieces[p][r], FLOOR)
            at = sum(sizes[:p])
            anchor[at : at + sizes[p], :] = start
            state[at : at + sizes[p], :] = start

        def step(_, c):
            iterate(whole, 1.0)
            return c

        lax.fori_loop(0, ITERS, step, 0)
        for b in range(per_row):
            lanes = slice(b * BLOCK, (b + 1) * BLOCK)

            @pl.when(slots[block + b] >= 0)
            def _():
                state[:, lanes] = anchor[:, lanes]

                def sub(_, c):
                    anchor[:, lanes] = state[:, lanes]

                    def step(_, c2):
                        iterate(lanes, 1.0 / SUB)
                        return c2

                    return lax.fori_loop(0, ITERS, step, c)

                lax.fori_loop(0, SUB, sub, 0)

        for s in range(n):
            outs[s][r] = state[s * group : (s + 1) * group, :]
        return carry

    lax.fori_loop(0, rows, one_row, 0)


def chemistry(classes, slots, pieces, tables, logs, n, parts, first, count, step, previous):
    cols = pieces[0].shape[2]
    group = sum(p.shape[1] for p in pieces) // n
    ordered = [] if previous is None else [previous]
    species = group * n
    reactions = logs.shape[1]
    base = first // step

    def fixed(shape):
        return pl.BlockSpec(
            shape, lambda i, *_: (0,) * len(shape), pipeline_mode=pl.Buffered(1)
        )

    return pl.pallas_call(
        functools.partial(chemistry_kernel, n, parts, first, len(ordered)),
        grid_spec=pltpu.PrefetchScalarGridSpec(
            num_scalar_prefetch=2,
            grid=(count // step,),
            in_specs=[pl.BlockSpec(memory_space=pl.ANY)] * len(ordered)
            + [pl.BlockSpec((step, p.shape[1], cols), lambda i, *_: (base + i, 0, 0)) for p in pieces]
            + [fixed(tables[0].shape), fixed(tables[1].shape), fixed(logs.shape)],
            out_specs=[pl.BlockSpec((step, group, cols), lambda i, *_: (i, 0, 0))] * n,
            scratch_shapes=[
                pltpu.VMEM((species, cols), jnp.float32),
                pltpu.VMEM((species, cols), jnp.float32),
                pltpu.VMEM((2 * species, cols), jnp.bfloat16),
                pltpu.VMEM((2 * reactions, cols), jnp.bfloat16),
                pltpu.VMEM((reactions, cols), jnp.float32),
            ],
        ),
        out_shape=[jax.ShapeDtypeStruct((count, group, cols), jnp.float32)] * n,
        compiler_params=pltpu.CompilerParams(vmem_limit_bytes=48 << 20),
        cost_estimate=pl.CostEstimate(
            flops=count * cols * species * reactions * 2 * 6 * ITERS,
            bytes_accessed=count * cols * species * 8,
            transcendentals=count * cols * (species + reactions) * ITERS,
        ),
    )(classes, slots, *ordered, *pieces, *tables, logs)


def assemble_kernel(n, per, aliased, ids, *rest):
    pieces = rest[aliased : aliased + n * per]
    out = rest[-1]
    group = out.shape[0]
    at = pl.program_id(0)
    for s in range(n):

        @pl.when(at == s)
        def _():
            mine = pieces[s * per : (s + 1) * per]

            def turn(q, carry):
                sp = pl.ds(pl.multiple_of(q * 8, 8), 8)
                parts = [p[:, sp, :] for p in mine]
                v = parts[0] if per == 1 else jnp.concatenate(parts, axis=0)
                out[sp] = jnp.swapaxes(v, 0, 1)
                return carry

            lax.fori_loop(0, group // 8, turn, 0)


def assemble(ids, pieces, per, previous, shape, n, row):
    group, rows, cols = shape
    own = rows // n // 8
    aliased = 0 if previous is None else 1
    row_block = row // 8
    specs = [
        pl.BlockSpec(p.shape, lambda i, ids: (0, 0, 0), pipeline_mode=pl.Buffered(1))
        for p in pieces
    ]
    return pl.pallas_call(
        functools.partial(assemble_kernel, n, per, aliased),
        grid_spec=pltpu.PrefetchScalarGridSpec(
            num_scalar_prefetch=1,
            grid=(n,),
            in_specs=[pl.BlockSpec(memory_space=pl.ANY)] * aliased + specs,
            out_specs=pl.BlockSpec(
                (group, 8, cols), lambda i, ids: (0, lax.rem(ids[0] + i, n) * own + row_block, 0)
            ),
        ),
        out_shape=jax.ShapeDtypeStruct(shape, jnp.float32),
        input_output_aliases={1: 0} if aliased else {},
        compiler_params=pltpu.CompilerParams(vmem_limit_bytes=32 << 20),
        cost_estimate=pl.CostEstimate(
            flops=group * 8 * n * cols, bytes_accessed=group * 8 * n * cols * 8, transcendentals=0
        ),
    )(ids, *([previous] if aliased else []), *pieces)


def halo(conc, winds):
    devices = lax.axis_size("region")
    up = [(i, i + 1) for i in range(devices - 1)]
    down = [(j, i) for i, j in up]
    length = conc.shape[1]
    last = jnp.concatenate([conc[:, length - HALO :], winds[:, length - HALO :]], axis=0)
    leading = jnp.concatenate([conc[:, :HALO], winds[:, :HALO]], axis=0)
    return lax.ppermute(last, "region", up), lax.ppermute(leading, "region", down)


def face_coefficients(winds):
    cx, cy = winds[0], winds[1]
    ax = 0.5 * (cx + jnp.pad(cx[1:], ((0, 1), (0, 0))))
    ay = 0.5 * (cy + jnp.pad(cy[:, 1:], ((0, 0), (0, 1))))
    left = 0.5 * cy

    def slope(a):
        return a * jnp.where(a >= 0.0, 0.5 * (1.0 - a), -0.5 * (1.0 + a))

    return jnp.stack(
        [
            ax,
            jnp.minimum(ax, 0.0),
            slope(ax),
            ay,
            jnp.minimum(ay, 0.0),
            slope(ay),
            jnp.minimum(left, 0.0),
            jnp.where(left >= 0.0, 0.0, slope(left)),
        ],
        axis=1,
    )


def per_device(conc, diffusion, courant_x, courant_y, log_rate, reactants, products, block_class, send_slot):
    n = lax.axis_size("species")
    group, rows, cols = conc.shape
    me = lax.axis_index("species")
    region = lax.axis_index("region")
    ids = jnp.stack([me, region, jnp.int32(lax.axis_size("region"))]).astype(jnp.int32)
    own = rows // n
    sizes = [16] * ((group - 16) // 16) + [8, 8]
    parts = len(sizes)

    winds = jnp.stack([courant_x, courant_y])
    top, bottom = halo(conc, winds)
    coef = face_coefficients(jnp.concatenate([top[group:], winds, bottom[group:]], axis=1))
    nu = jnp.broadcast_to(diffusion[:, None], (group, cols))
    held = [[None] * parts for _ in range(n)]
    for j in range(parts):
        sent = transport(ids, conc, top, bottom, nu, coef, n, sizes[j], sum(sizes[:j]))
        held[0][j] = sent[0]
        for s in range(1, n):
            held[s][j] = lax.ppermute(sent[s], "species", [(i, (i + s) % n) for i in range(n)])

    order = lax.rem(me - jnp.arange(n) + n, n)
    reacts = jnp.take(reactants.reshape(n, group, -1), order, axis=0).reshape(n * group, -1)
    makes = jnp.take(products.T.reshape(n, group, -1), order, axis=0).reshape(n * group, -1)
    reacts, makes = reacts.astype(jnp.bfloat16), makes.astype(jnp.bfloat16)
    first_table = jnp.concatenate([reacts.T, reacts.T], axis=1)
    second = jnp.concatenate([makes, reacts], axis=0)
    second_table = jnp.concatenate([second, second], axis=1)
    logs = jnp.broadcast_to(log_rate[:, :, None], log_rate.shape + (BLOCK,))

    pieces = [held[s][j] for s in range(n) for j in range(parts)]
    step = 2
    counts = [2, 6] + [8] * (own // 8 - 1)
    result, at, waiting, made = None, 0, [], [None]
    for count in counts:
        made = chemistry(
            block_class, send_slot, pieces, (first_table, second_table), logs, n, parts, at, count, step, made[0]
        )
        back = [made[0]]
        for s in range(1, n):
            back.append(lax.ppermute(made[s], "species", [(i, (i - s) % n) for i in range(n)]))
        waiting.append(back)
        at += count
        if at % 8 == 0:
            done = [w[s] for s in range(n) for w in waiting]
            result = assemble(ids, done, len(waiting), result, conc.shape, n, at - 8)
            waiting = []
    return result


def solution(mesh):
    in_specs = (
        P("species", "region", None),
        P("species"),
        P("region", None),
        P("region", None),
        P(),
        P(),
        P(),
        P(("region", "species")),
        P(("region", "species")),
    )
    out_specs = P("species", "region", None)

    return jax.shard_map(per_device, mesh=mesh, in_specs=in_specs, out_specs=out_specs, check_vma=False)
```
